32 devices in a mesh: dp: 4 (over z), seq: 4 (over x, core), mp: 2 (over y).
Axes of the slice: x: 2, y: 2, z: 4, core: 2. Of those that a mesh axis runs over, the one named last changes fastest.
Arguments:
- tokens: bfloat16 [4, 1024, 1536], P('dp', 'seq'), may hold values from -6 to 6
- doc_lengths: int32 [4, 8], P('dp'), may hold values from 1 to 512, 1024 in all within a row
- attention_gain: float32 [1536], replicated, may hold values from 0.5 to 1.5
- query_weight: bfloat16 [1536, 1536], P(('dp', 'seq'), 'mp'), may hold values from -0.15625 to 0.15625
- key_weight: bfloat16 [1536, 1536], P(('dp', 'seq'), 'mp'), may hold values from -0.15625 to 0.15625
- value_weight: bfloat16 [1536, 1536], P(('dp', 'seq'), 'mp'), may hold values from -0.15625 to 0.15625
- output_weight: bfloat16 [1536, 1536], P(('dp', 'seq'), 'mp'), may hold values from -0.15625 to 0.15625
- head_gain: float32 [128], replicated, may hold values from 0.5 to 1.5
- lambda_vectors: float32 [4, 64], replicated, may hold values from -0.05 to 0.05
- feedforward_gain: float32 [1536], replicated, may hold values from 0.5 to 1.5
- gate_weight: bfloat16 [1536, 4096], P(('dp', 'seq'), 'mp'), may hold values from -0.15625 to 0.15625
- up_weight: bfloat16 [1536, 4096], P(('dp', 'seq'), 'mp'), may hold values from -0.15625 to 0.15625
- down_weight: bfloat16 [1536, 4096], P(('dp', 'seq'), 'mp'), may hold values from -0.09375 to 0.09375
- cotangent: bfloat16 [4, 1024, 1536], P('dp', 'seq'), may hold values from -6 to 6
Outputs:
- result: bfloat16 [4, 1024, 1536], P('dp', 'seq')
- tokens_grad: bfloat16 [4, 1024, 1536], P('dp', 'seq')
- attention_gain_grad: float32 [1536], replicated
- query_weight_grad: float32 [1536, 1536], P(('dp', 'seq'), 'mp')
- key_weight_grad: float32 [1536, 1536], P(('dp', 'seq'), 'mp')
- value_weight_grad: float32 [1536, 1536], P(('dp', 'seq'), 'mp')
- output_weight_grad: float32 [1536, 1536], P(('dp', 'seq'), 'mp')
- head_gain_grad: float32 [128], replicated
- lambda_grad: float32 [4, 64], replicated
- feedforward_gain_grad: float32 [1536], replicated
- gate_weight_grad: float32 [1536, 4096], P(('dp', 'seq'), 'mp')
- up_weight_grad: float32 [1536, 4096], P(('dp', 'seq'), 'mp')
- down_weight_grad: float32 [1536, 4096], P(('dp', 'seq'), 'mp')
The draws below stay inside these ranges and needn't reach their ends.
Inputs may be any that keep to these rules, and one draw needn't show every extreme that they name: `doc_lengths`: each row's 8 entries are the lengths of its consecutive documents in order and sum to 1024; the last entry is the padding at the row's end.
All inputs are finite; a program needn't handle non-finite values.
Results may differ from the reference program's by a relative error of at most 0.015.
Values may be sent and summed in bfloat16 or wider, within the bound.
No kernel may reach another device: no remote copies, remote signals or barrier semaphores. Data moves between devices by JAX's collectives and lax.ppermute only.
A program may use at most 192 MiB of HBM per device.

```python
import math
import jax
import jax.numpy as jnp
import numpy as np
from jax import lax

D = 1536
HEADS = 12
HALF = 64
FF = 4096
DOCS = 8
LEN = 1024
ROWS = 4
MOST_DOC = 512


def raised(result, key, source, target, blocks, factor):
    def block_of(dim):
        return (jnp.arange(result.shape[dim]) // (result.shape[dim] // blocks)).reshape((-1,) + (1,) * (result.ndim - 1 - dim))

    first = jax.random.permutation(key, blocks)[block_of(target)]
    second = (block_of(target) + blocks // 2) % blocks
    return jnp.where((block_of(source) == first) | (block_of(source) == second), factor * result, result)


def levels(own_key, shape, pieces, smallest, top_value):
    def one(axis_at, parts):
        heights = jax.random.uniform(jax.random.fold_in(jax.random.fold_in(own_key, 6), axis_at), (parts,), jnp.float32, smallest / len(pieces), top_value / len(pieces))
        return jnp.repeat(jnp.exp(heights), shape[axis_at] // parts).reshape((-1,) + (1,) * (len(shape) - axis_at - 1))

    level = one(*pieces[0])
    for cut in pieces[1:]:
        level = level * one(*cut)
    return level


def split_up(count, total, bound, skew):
    loads = [(1 << 20) // math.isqrt(rank ** skew) + 1 for rank in range(2, count + 1)]
    surplus, holding = total - bound - (count - 1), [1] * (count - 1)
    while surplus > 0:
        movable = [i for i in range(count - 1) if holding[i] < bound]
        mass, budget = sum([loads[i] for i in movable]), surplus
        for i in movable:
            more = min(bound - holding[i], max(1, budget * loads[i] // mass), surplus)
            holding[i] = holding[i] + more
            surplus = surplus - more
    return np.array([bound] + holding)


def ragged_sizes(stream_key, count, total, limit, skew):
    if count == 2:
        one = jax.random.randint(stream_key, (), max(1, total - limit), min(limit, total - 1) + 1)
        return jnp.stack([one, total - one])
    tallies = jnp.asarray(split_up(count, total, limit, skew), jnp.int32)
    couples = (count - 1) // 2
    donor, receiver = tallies[1:1 + 2 * couples:2], tallies[2:2 + 2 * couples:2]
    slack = jnp.minimum(donor - 1, limit - receiver)
    shifted = jax.random.randint(jax.random.fold_in(stream_key, 1), (couples,), 0, 1 << 20) % (slack + 1)
    tallies = tallies.at[1:1 + 2 * couples:2].set(donor - shifted).at[2:2 + 2 * couples:2].set(receiver + shifted)
    return tallies[jax.random.permutation(jax.random.fold_in(stream_key, 2), count)]


def gaussian(key, dims, scale, reach, shards=(), kind=jnp.bfloat16):
    entries = jax.random.normal(key, dims, jnp.float32) * scale
    if len(shards) > 0:
        entries = levels(key, dims, shards, -0.22, 0.18) * entries
    return jnp.clip(entries, min=-reach, max=reach).astype(kind)


def heavy_noise(stream_key, dims, spread, reach, cuts, heavy, held_as=jnp.bfloat16):
    array = spread * jax.random.normal(stream_key, dims, jnp.float32)
    if cuts:
        array = array * levels(stream_key, dims, cuts, -0.22, 0.18)
    return jnp.clip(raised(array, jax.random.fold_in(stream_key, 3), *heavy), -reach, reach).astype(held_as)


def setup_inputs(seed: int = 0) -> dict:
    arg_keys = jax.random.split(jax.random.key(seed), 15)
    return {
        "tokens": gaussian(arg_keys[0], (ROWS, LEN, D), 1.0, 6.0, ((0, 4), (1, 4))),
        "doc_lengths": jax.vmap(lambda own: ragged_sizes(own, DOCS, LEN, MOST_DOC, 2))(jax.random.split(arg_keys[1], ROWS)).reshape((ROWS, DOCS)).astype(jnp.int32),
        "attention_gain": jnp.clip(1.0 + 0.1 * jax.random.normal(arg_keys[2], (D,), jnp.float32), 0.5, 1.5),
        "query_weight": gaussian(arg_keys[3], (D, 2 * HEADS * HALF), D ** -0.5, 0.15625, ((0, 16), (1, 2))),
        "key_weight": gaussian(arg_keys[4], (D, 2 * HEADS * HALF), D ** -0.5, 0.15625, ((0, 16), (1, 2))),
        "value_weight": gaussian(arg_keys[5], (D, 2 * HEADS * HALF), D ** -0.5, 0.15625, ((0, 16), (1, 2))),
        "output_weight": gaussian(arg_keys[6], (D, 2 * HEADS * HALF), (2 * HEADS * HALF) ** -0.5, 0.15625, ((0, 16), (1, 2))),
        "head_gain": jnp.clip(1.0 + 0.1 * jax.random.normal(arg_keys[7], (2 * HALF,), jnp.float32), 0.5, 1.5),
        "lambda_vectors": jnp.clip(jax.random.uniform(arg_keys[8], (4, HALF), jnp.float32, -0.05, 0.05), -0.05, 0.05),
        "feedforward_gain": jnp.clip(1.0 + 0.1 * jax.random.normal(arg_keys[9], (D,), jnp.float32), 0.5, 1.5),
        "gate_weight": gaussian(arg_keys[10], (D, FF), D ** -0.5, 0.15625, ((0, 16), (1, 2))),
        "up_weight": gaussian(arg_keys[11], (D, FF), D ** -0.5, 0.15625, ((0, 16), (1, 2))),
        "down_weight": gaussian(arg_keys[12], (D, FF), FF ** -0.5, 0.09375, ((0, 16), (1, 2))),
        "cotangent": heavy_noise(arg_keys[13], (ROWS, LEN, D), 1.0, 6.0, ((0, 4), (1, 4)), (0, 2, 4, 2.0)),
    }


EPSILON = 1e-05
LAMBDA_INIT = 0.2
OUTPUT_SCALE = 1.0 - LAMBDA_INIT
NEGATIVE = -1e+30
HIGHEST = lax.Precision.HIGHEST

@jax.custom_vjp
def low(v):
    return lax.optimization_barrier(v.astype(jnp.bfloat16)).astype(jnp.float32)

@jax.custom_vjp
def low_back(v):
    return v

def low_keep(v):
    return (low(v), None)

def low_pass(kept, grad):
    return (grad,)

def back_keep(v):
    return (v, None)

def back_low(kept, grad):
    return (low(grad),)
low.defvjp(low_keep, low_pass)
low_back.defvjp(back_keep, back_low)

def tables(doc_lengths, length):
    doc_count = doc_lengths.shape[0]
    doc_ends = jnp.cumsum(doc_lengths).astype(jnp.int32)
    places = jnp.arange(length, dtype=jnp.int32)
    segment = lax.optimization_barrier(jnp.sum((places[:, None] >= doc_ends[None, :]).astype(jnp.int32), axis=1)).astype(jnp.int32)
    matched = segment[:, None] == jnp.arange(doc_count, dtype=jnp.int32)[None, :]
    doc_start = lax.optimization_barrier(jnp.sum(jnp.where(matched, (doc_ends - doc_lengths)[None, :], 0), axis=1)).astype(jnp.int32)
    return (segment, (places - doc_start).astype(jnp.int32), segment < doc_count - 1)

def rotary(position, half_width):
    pair_count = half_width // 2
    frequency = jnp.exp(jnp.arange(pair_count, dtype=jnp.float32) * (-2.0 * math.log(10000.0) / half_width))
    angles = position.astype(jnp.float32)[:, None] * frequency[None, :]
    return (jnp.cos(angles), jnp.sin(angles))

def rotate(values, cos_table, sin_table):
    middle = values.shape[-1] // 2
    first_half = values[..., :middle]
    second_half = values[..., middle:]
    return jnp.concatenate([first_half * cos_table - second_half * sin_table, second_half * cos_table + first_half * sin_table], axis=-1)

def rms_norm(values, gain):
    return values * lax.rsqrt(lax.optimization_barrier(jnp.mean(values * values, axis=-1, keepdims=True)) + EPSILON) * gain

def project(values, weight):
    return jnp.einsum('rld,dx->rlx', values, weight, precision=HIGHEST)

def attend_head(element, allowed, lam_value):
    query_pair, key_pair, value_head = element
    score_scale = HALF ** (-0.5)
    results = []
    for half_index in range(2):
        scores = low_back(jnp.dot(query_pair[half_index], key_pair[half_index].T, precision=HIGHEST)) * score_scale
        scores = jnp.where(allowed, scores, NEGATIVE)
        weights_soft = jax.nn.softmax(scores, axis=-1)
        results.append(low_back(jnp.dot(low(weights_soft), value_head, precision=HIGHEST)))
    return results[0] - lam_value * results[1]

def attend_row(element, lam_value):
    query_rows, key_rows, value_rows, segment = element
    length = segment.shape[0]
    places = jnp.arange(length, dtype=jnp.int32)
    allowed = (segment[:, None] == segment[None, :]) & (places[:, None] >= places[None, :])
    query_heads = jnp.transpose(query_rows.reshape(length, HEADS, 2, HALF), (1, 2, 0, 3))
    key_heads = jnp.transpose(key_rows.reshape(length, HEADS, 2, HALF), (1, 2, 0, 3))
    value_heads = jnp.transpose(value_rows, (1, 0, 2))
    head_step = jax.checkpoint(lambda inner_element: attend_head(inner_element, allowed, lam_value))
    return lax.map(head_step, (query_heads, key_heads, value_heads))

def forward_layer(x_rows, attention_gain, query_weight, key_weight, value_weight, output_weight, head_gain, lambda_vectors, feedforward_gain, gate_weight, up_weight, down_weight, segment, position):
    row_count, length, model_width = x_rows.shape
    lam_value = jnp.exp(jnp.sum(lambda_vectors[0] * lambda_vectors[1])) - jnp.exp(jnp.sum(lambda_vectors[2] * lambda_vectors[3])) + LAMBDA_INIT
    normed_one = low(rms_norm(x_rows, attention_gain))
    cos_table, sin_table = jax.vmap(lambda pos_row: rotary(pos_row, HALF))(position)
    cos_table = cos_table[:, :, None, :]
    sin_table = sin_table[:, :, None, :]
    query_rows = low_back(project(normed_one, query_weight)).reshape(row_count, length, 2 * HEADS, HALF)
    query_rows = low(rotate(query_rows, cos_table, sin_table)).reshape(row_count, length, 2 * HEADS * HALF)
    key_rows = low_back(project(normed_one, key_weight)).reshape(row_count, length, 2 * HEADS, HALF)
    key_rows = low(rotate(key_rows, cos_table, sin_table)).reshape(row_count, length, 2 * HEADS * HALF)
    value_rows = low(low_back(project(normed_one, value_weight))).reshape(row_count, length, HEADS, 2 * HALF)
    mixture = lax.map(lambda element: attend_row(element, lam_value), (query_rows, key_rows, value_rows, segment))
    inverse_head = lax.rsqrt(lax.optimization_barrier(jnp.mean(mixture * mixture, axis=-1, keepdims=True)) + EPSILON)
    normed_head = low(mixture * inverse_head * head_gain * OUTPUT_SCALE)
    flattened = jnp.transpose(normed_head, (0, 2, 1, 3)).reshape(row_count, length, 2 * HEADS * HALF)
    hidden_state = x_rows + low_back(jnp.einsum('rlx,dx->rld', flattened, output_weight, precision=HIGHEST))
    normed_two = low(rms_norm(hidden_state, feedforward_gain))
    gate_value = low_back(project(normed_two, gate_weight))
    up_value = low_back(project(normed_two, up_weight))
    inner_act = low(jax.nn.silu(gate_value) * up_value)
    return hidden_state + low_back(jnp.einsum('rlf,df->rld', inner_act, down_weight, precision=HIGHEST))

def reference(tokens, doc_lengths, attention_gain, query_weight, key_weight, value_weight, output_weight, head_gain, lambda_vectors, feedforward_gain, gate_weight, up_weight, down_weight, cotangent):
    segment, position, usable = jax.vmap(lambda lengths_row: tables(lengths_row, LEN))(doc_lengths)
    inputs = (tokens.astype(jnp.float32), attention_gain.astype(jnp.float32), query_weight.astype(jnp.float32), key_weight.astype(jnp.float32), value_weight.astype(jnp.float32), output_weight.astype(jnp.float32), head_gain.astype(jnp.float32), lambda_vectors.astype(jnp.float32), feedforward_gain.astype(jnp.float32), gate_weight.astype(jnp.float32), up_weight.astype(jnp.float32), down_weight.astype(jnp.float32))
    out_value, pull_back = jax.vjp(lambda *params: forward_layer(*params, segment, position), *inputs)
    gradients = pull_back(cotangent.astype(jnp.float32) * usable[:, :, None].astype(jnp.float32))
    return (out_value.astype(jnp.bfloat16), gradients[0].astype(jnp.bfloat16), gradients[1], gradients[2], gradients[3], gradients[4], gradients[5], gradients[6], gradients[7], gradients[8], gradients[9], gradients[10], gradients[11])
```

```python
import functools
import math

import jax
import jax.numpy as jnp
from jax import lax
from jax.experimental import pallas as pl
from jax.experimental.pallas import tpu as pltpu
from jax.sharding import PartitionSpec as P

EPSILON = 1e-05
LAMBDA_INIT = 0.2
OUTPUT_SCALE = 1.0 - LAMBDA_INIT
NEGATIVE = -1e30
MOST_DOC = 512
F32 = jnp.float32
BF16 = jnp.bfloat16


def dot(a, b):
    return lax.dot_general(a, b, (((1,), (0,)), ((), ())), preferred_element_type=F32)


def dot_nt(a, b):
    return lax.dot_general(a, b, (((1,), (1,)), ((), ())), preferred_element_type=F32)


def dot_tn(a, b):
    return lax.dot_general(a, b, (((0,), (0,)), ((), ())), preferred_element_type=F32)


def full_spec(shape):
    return pl.BlockSpec(shape, lambda *_: (0,) * len(shape))


def cost(flops, moved, special=0):
    return pl.CostEstimate(flops=int(flops), bytes_accessed=int(moved), transcendentals=int(special))


def swap_halves(values, quarter):
    width = 4 * quarter
    lane = lax.broadcasted_iota(jnp.int32, values.shape, 1)
    ahead = pltpu.roll(values, width - quarter, 1)
    behind = pltpu.roll(values, quarter, 1)
    return jnp.where((lane % (2 * quarter)) < quarter, ahead, behind)


def qkv_kernel(rotated, head_width, x_ref, gain_ref, cos_ref, sin_ref, w_ref, out_ref, normed_ref):
    step = pl.program_id(0)

    @pl.when(step == 0)
    def _():
        values = x_ref[...].astype(F32)
        inverse = lax.rsqrt(jnp.mean(values * values, axis=-1, keepdims=True) + EPSILON)
        normed_ref[...] = (values * inverse * gain_ref[...]).astype(BF16)

    product = dot(normed_ref[...], w_ref[...])

    @pl.when(step < rotated)
    def _():
        for start in range(0, product.shape[1], head_width):
            piece = product[:, start : start + head_width]
            turned = piece * cos_ref[...] + swap_halves(piece, head_width // 4) * sin_ref[...]
            out_ref[:, start : start + head_width] = turned.astype(BF16)

    @pl.when(step >= rotated)
    def _():
        out_ref[...] = product.astype(BF16)


def project_qkv(x, gain, cos_table, sin_table, weights, width, head_width):
    length, model = x.shape
    tile = 256
    return pl.pallas_call(
        functools.partial(qkv_kernel, 2 * width // tile, head_width),
        grid=(3 * width // tile,),
        in_specs=[
            full_spec((length, model)),
            full_spec((1, model)),
            full_spec((length, head_width)),
            full_spec((length, head_width)),
            pl.BlockSpec((model, tile), lambda j: (0, j)),
        ],
        out_specs=[
            pl.BlockSpec((length, tile), lambda j: (0, j)),
            full_spec((length, model)),
        ],
        out_shape=[
            jax.ShapeDtypeStruct((length, 3 * width), BF16),
            jax.ShapeDtypeStruct((length, model), BF16),
        ],
        cost_estimate=cost(6 * length * model * width, 6 * model * width + 8 * length * width),
        name="qkv_project",
    )(x, gain, cos_table, sin_table, weights)


def masks_of(seg_q, seg_k_ref, blocks):
    length = seg_q.shape[0]
    allowed = []
    for b in range(blocks):
        same = seg_q == seg_k_ref[b : b + 1, :]
        if b == 0:
            rows = lax.broadcasted_iota(jnp.int32, (length, length), 0)
            columns = lax.broadcasted_iota(jnp.int32, (length, length), 1)
            same = same & (rows >= columns)
        allowed.append(same)
    return allowed


def attend_kernel(blocks, *refs):
    lam_ref, seg_q_ref, seg_k_ref, gain_ref, q_ref = refs[:5]
    k_refs = refs[5 : 5 + blocks]
    v_refs = refs[5 + blocks : 5 + 2 * blocks]
    normed_ref, mixture_ref, second_ref, logsum_ref = refs[5 + 2 * blocks :]
    half = q_ref.shape[1] // 2
    scale = half ** (-0.5)
    allowed = masks_of(seg_q_ref[...], seg_k_ref, blocks)
    outputs = []
    for j in range(2):
        cut = slice(j * half, (j + 1) * half)
        query = q_ref[:, cut]
        scores = [
            jnp.where(allowed[b], dot_nt(query, k_refs[b][:, cut]) * scale, NEGATIVE)
            for b in range(blocks)
        ]
        highest = functools.reduce(
            jnp.maximum, [jnp.max(s, axis=-1, keepdims=True) for s in scores]
        )
        exponents = [jnp.exp(s - highest) for s in scores]
        total = sum(jnp.sum(e, axis=-1, keepdims=True) for e in exponents)
        inverse = 1.0 / total
        outputs.append(
            sum(dot((exponents[b] * inverse).astype(BF16), v_refs[b][...]) for b in range(blocks))
        )
        logsum_ref[0, :, j : j + 1] = highest + jnp.log(total)
    mixture = outputs[0] - lam_ref[0, 0] * outputs[1]
    inverse_head = lax.rsqrt(jnp.mean(mixture * mixture, axis=-1, keepdims=True) + EPSILON)
    normed_ref[...] = (mixture * inverse_head * (gain_ref[...] * OUTPUT_SCALE)).astype(BF16)
    mixture_ref[...] = mixture
    second_ref[...] = outputs[1]


def attend(lam, seg_q, seg_k, head_gain, qkv, prior, heads, head_width):
    length = qkv.shape[0]
    blocks = seg_k.shape[0]
    block = (length, head_width)

    def at(first):
        return pl.BlockSpec(block, lambda h: (0, first + h))

    width = heads * head_width
    return pl.pallas_call(
        functools.partial(attend_kernel, blocks),
        grid=(heads,),
        in_specs=[
            pl.BlockSpec(memory_space=pltpu.SMEM),
            full_spec(seg_q.shape),
            full_spec(seg_k.shape),
            full_spec(head_gain.shape),
            at(0),
            at(heads),
            *[at(0) for _ in prior],
            at(2 * heads),
            *[at(heads) for _ in prior],
        ],
        out_specs=[at(0), at(0), at(0), pl.BlockSpec((1, length, 2), lambda h: (h, 0, 0))],
        out_shape=[
            jax.ShapeDtypeStruct((length, width), BF16),
            jax.ShapeDtypeStruct((length, width), F32),
            jax.ShapeDtypeStruct((length, width), F32),
            jax.ShapeDtypeStruct((heads, length, 2), F32),
        ],
        cost_estimate=cost(
            8 * heads * length * length * blocks * head_width,
            length * width * (2 + 4 * blocks + 10),
            2 * heads * length * length * blocks,
        ),
        name="attend_forward",
    )(lam, seg_q, seg_k, head_gain, qkv, qkv, *prior, qkv, *prior)


def feed_kernel(
    x_ref, own_ref, other_ref, gain_ref, cot_ref, usable_ref, gate_ref, up_ref, down_ref,
    hidden_ref, normed_ref, low_ref, inner_ref, grad_gate_ref, grad_up_ref,
    part_ref, back_ref, gain_part_ref, sum_out, sum_back, inverse_ref,
):
    step = pl.program_id(0)
    gain = gain_ref[...]

    @pl.when(step == 0)
    def _():
        hidden = x_ref[...].astype(F32) + (own_ref[...].astype(F32) + other_ref[...].astype(F32))
        inverse = lax.rsqrt(jnp.mean(hidden * hidden, axis=-1, keepdims=True) + EPSILON)
        hidden_ref[...] = hidden
        inverse_ref[...] = inverse
        normed_ref[...] = (hidden * inverse * gain).astype(BF16)
        low_ref[...] = (cot_ref[...].astype(F32) * usable_ref[...]).astype(BF16)
        sum_out[...] = jnp.zeros_like(sum_out)
        sum_back[...] = jnp.zeros_like(sum_back)

    normed = normed_ref[...]
    gate = dot(normed, gate_ref[...])
    up = dot(normed, up_ref[...])
    grad_inner = dot(low_ref[...], down_ref[...])
    sigmoid = jax.nn.sigmoid(gate)
    silu = gate * sigmoid
    inner = (silu * up).astype(BF16)
    grad_gate = (grad_inner * up * (sigmoid * (1.0 + gate * (1.0 - sigmoid)))).astype(BF16)
    grad_up = (grad_inner * silu).astype(BF16)
    inner_ref[...] = inner
    grad_gate_ref[...] = grad_gate
    grad_up_ref[...] = grad_up
    sum_out[...] += dot_nt(inner, down_ref[...])
    sum_back[...] += dot_nt(grad_gate, gate_ref[...]) + dot_nt(grad_up, up_ref[...])

    @pl.when(step == pl.num_programs(0) - 1)
    def _():
        part_ref[...] = sum_out[...].astype(BF16)
        inverse = inverse_ref[...]
        unit = hidden_ref[...] * inverse
        grad = sum_back[...]
        weighed = gain * grad
        gain_part_ref[...] = jnp.sum(grad * unit, axis=0, keepdims=True)
        centre = jnp.mean(weighed * unit, axis=-1, keepdims=True)
        back_ref[...] = (inverse * (weighed - unit * centre)).astype(BF16)


def feed_forward(x, own, other, gain, cotangent, usable, weights, hidden_units):
    length, model = x.shape
    tile = 256
    tiles = hidden_units // tile
    whole = (length, model)

    def weight_at(first):
        return pl.BlockSpec((model, tile), lambda j: (0, first * tiles + j))

    column = pl.BlockSpec((length, tile), lambda j: (0, j))
    return pl.pallas_call(
        feed_kernel,
        grid=(tiles,),
        in_specs=[
            full_spec(whole), full_spec(whole), full_spec(whole), full_spec((1, model)),
            full_spec(whole), full_spec((length, 1)), weight_at(0), weight_at(1), weight_at(2),
        ],
        out_specs=[
            full_spec(whole), full_spec(whole), full_spec(whole), column, column, column,
            full_spec(whole), full_spec(whole), full_spec((1, model)),
        ],
        out_shape=[
            jax.ShapeDtypeStruct(whole, F32),
            jax.ShapeDtypeStruct(whole, BF16),
            jax.ShapeDtypeStruct(whole, BF16),
            *[jax.ShapeDtypeStruct((length, hidden_units), BF16)] * 3,
            jax.ShapeDtypeStruct(whole, BF16),
            jax.ShapeDtypeStruct(whole, BF16),
            jax.ShapeDtypeStruct((1, model), F32),
        ],
        scratch_shapes=[
            pltpu.VMEM(whole, F32), pltpu.VMEM(whole, F32), pltpu.VMEM((length, 1), F32),
        ],
        cost_estimate=cost(
            12 * length * model * hidden_units, 6 * model * hidden_units + 20 * length * model
        ),
        name="feed_forward",
    )(x, own, other, gain, cotangent, usable, weights, weights, weights)


def attend_back_kernel(blocks, *refs):
    (lam_ref, seg_q_ref, seg_k_ref, gain_ref, cos_ref, sin_ref, low_ref, own_ref, other_ref,
     out_weight_ref, mixture_ref, second_ref, logsum_ref, q_ref) = refs[:14]
    k_refs = refs[14 : 14 + blocks]
    v_refs = refs[14 + blocks : 14 + 2 * blocks]
    grad_hidden_ref, hidden_low_ref, grad_q_ref, own_kv_ref = refs[14 + 2 * blocks : 18 + 2 * blocks]
    prior_kv_refs = refs[18 + 2 * blocks : 17 + 3 * blocks]
    gain_part_ref, lam_part_ref = refs[17 + 3 * blocks :]
    step = pl.program_id(0)

    @pl.when(step == 0)
    def _():
        grad_hidden = low_ref[...].astype(F32) + (
            own_ref[...].astype(F32) + other_ref[...].astype(F32)
        )
        grad_hidden_ref[...] = grad_hidden
        hidden_low_ref[...] = grad_hidden.astype(BF16)
        gain_part_ref[...] = jnp.zeros_like(gain_part_ref)
        lam_part_ref[...] = jnp.zeros_like(lam_part_ref)

    head_width = q_ref.shape[1]
    half = head_width // 2
    scale = half ** (-0.5)
    lam = lam_ref[0, 0]
    grad_head = dot(hidden_low_ref[...], out_weight_ref[...])
    mixture = mixture_ref[...]
    inverse_head = lax.rsqrt(jnp.mean(mixture * mixture, axis=-1, keepdims=True) + EPSILON)
    unit_head = mixture * inverse_head
    gain_part_ref[...] += jnp.sum(grad_head * unit_head, axis=0, keepdims=True) * OUTPUT_SCALE
    weighed = gain_ref[...] * OUTPUT_SCALE * grad_head
    centre_head = jnp.mean(weighed * unit_head, axis=-1, keepdims=True)
    grad_mixture = inverse_head * (weighed - unit_head * centre_head)
    lam_part_ref[...] -= jnp.sum(grad_mixture * second_ref[...], axis=0, keepdims=True)
    grads = (grad_mixture.astype(BF16), (-lam * grad_mixture).astype(BF16))
    allowed = masks_of(seg_q_ref[...], seg_k_ref, blocks)
    grad_queries = []
    grad_keys = [[] for _ in range(blocks)]
    grad_values = [0.0] * blocks
    for j in range(2):
        cut = slice(j * half, (j + 1) * half)
        query = q_ref[:, cut]
        grad_out = grads[j]
        logsum = logsum_ref[0, :, j : j + 1]
        soft, grad_soft = [], []
        for b in range(blocks):
            scores = dot_nt(query, k_refs[b][:, cut]) * scale
            soft.append(jnp.exp(jnp.where(allowed[b], scores - logsum, NEGATIVE)))
            grad_soft.append(dot_nt(grad_out, v_refs[b][...]))
            grad_values[b] = grad_values[b] + dot_tn(soft[b].astype(BF16), grad_out)
        centre = sum(jnp.sum(soft[b] * grad_soft[b], axis=-1, keepdims=True) for b in range(blocks))
        grad_query = 0.0
        for b in range(blocks):
            grad_scores = (scale * soft[b] * (grad_soft[b] - centre)).astype(BF16)
            grad_query = grad_query + dot(grad_scores, k_refs[b][:, cut])
            grad_keys[b].append(dot_tn(grad_scores, query))
        grad_queries.append(grad_query)
    grad_query = jnp.concatenate(grad_queries, axis=1)
    turned = grad_query * cos_ref[...] - swap_halves(grad_query, head_width // 4) * sin_ref[...]
    grad_q_ref[...] = turned.astype(BF16)
    for b, ref in enumerate((own_kv_ref, *prior_kv_refs)):
        ref[:, :head_width] = jnp.concatenate(grad_keys[b], axis=1).astype(ref.dtype)
        ref[:, head_width:] = grad_values[b].astype(ref.dtype)


def attend_back(
    lam, seg_q, seg_k, head_gain, cos_table, sin_table, grad_low, own, other, weights,
    mixture, second, logsum, qkv, prior, heads, head_width,
):
    length, model = grad_low.shape
    blocks = seg_k.shape[0]
    whole = (length, model)
    width = heads * head_width

    def at(first):
        return pl.BlockSpec((length, head_width), lambda h: (0, first + h))

    pair = pl.BlockSpec((length, 2 * head_width), lambda h: (0, h))
    return pl.pallas_call(
        functools.partial(attend_back_kernel, blocks),
        grid=(heads,),
        in_specs=[
            pl.BlockSpec(memory_space=pltpu.SMEM),
            full_spec(seg_q.shape), full_spec(seg_k.shape), full_spec(head_gain.shape),
            full_spec((length, head_width)), full_spec((length, head_width)),
            full_spec(whole), full_spec(whole), full_spec(whole),
            pl.BlockSpec((model, head_width), lambda h: (0, 3 * heads + h)),
            at(0), at(0), pl.BlockSpec((1, length, 2), lambda h: (h, 0, 0)),
            at(0),
            at(heads), *[at(0) for _ in prior],
            at(2 * heads), *[at(heads) for _ in prior],
        ],
        out_specs=[
            full_spec(whole), full_spec(whole), at(0), pair, *[pair for _ in prior],
            full_spec((1, head_width)), full_spec((1, head_width)),
        ],
        out_shape=[
            jax.ShapeDtypeStruct(whole, F32),
            jax.ShapeDtypeStruct(whole, BF16),
            jax.ShapeDtypeStruct((length, width), BF16),
            jax.ShapeDtypeStruct((length, 2 * width), F32),
            *[jax.ShapeDtypeStruct((length, 2 * width), BF16) for _ in prior],
            jax.ShapeDtypeStruct((1, head_width), F32),
            jax.ShapeDtypeStruct((1, head_width), F32),
        ],
        cost_estimate=cost(
            24 * heads * length * length * blocks * head_width + 2 * length * model * width,
            2 * model * width + 24 * length * model,
            2 * heads * length * length * blocks,
        ),
        name="attend_backward",
    )(
        lam, seg_q, seg_k, head_gain, cos_table, sin_table, grad_low, own, other, weights,
        mixture, second, logsum, qkv, qkv, *prior, qkv, *prior,
    )


def input_back_kernel(
    arrivals, *refs,
):
    x_ref, gain_ref, cos_ref, sin_ref, grad_q_ref, own_ref = refs[:6]
    arrival_refs = refs[6 : 6 + arrivals]
    wq_ref, wk_ref, wv_ref, grad_k_ref, grad_v_ref, back_ref, gain_part_ref, total = refs[6 + arrivals :]
    step = pl.program_id(0)
    head_width = grad_q_ref.shape[1]
    pair = own_ref[...]
    for ref in arrival_refs:
        pair = pair + ref[...].astype(F32)
    grad_key = pair[:, :head_width]
    turned = grad_key * cos_ref[...] - swap_halves(grad_key, head_width // 4) * sin_ref[...]
    grad_k = turned.astype(BF16)
    grad_v = pair[:, head_width:].astype(BF16)
    grad_k_ref[...] = grad_k
    grad_v_ref[...] = grad_v

    @pl.when(step == 0)
    def _():
        total[...] = jnp.zeros_like(total)

    total[...] += (
        dot_nt(grad_q_ref[...], wq_ref[...])
        + dot_nt(grad_k, wk_ref[...])
        + dot_nt(grad_v, wv_ref[...])
    )

    @pl.when(step == pl.num_programs(0) - 1)
    def _():
        values = x_ref[...].astype(F32)
        inverse = lax.rsqrt(jnp.mean(values * values, axis=-1, keepdims=True) + EPSILON)
        unit = values * inverse
        grad = total[...]
        weighed = gain_ref[...] * grad
        gain_part_ref[...] = jnp.sum(grad * unit, axis=0, keepdims=True)
        centre = jnp.mean(weighed * unit, axis=-1, keepdims=True)
        back_ref[...] = (inverse * (weighed - unit * centre)).astype(BF16)


def input_back(x, gain, cos_table, sin_table, grad_q, own, arrived, weights, heads, head_width):
    length, model = x.shape
    width = heads * head_width
    whole = (length, model)

    def weight_at(first):
        return pl.BlockSpec((model, head_width), lambda h: (0, first * heads + h))

    column = pl.BlockSpec((length, head_width), lambda h: (0, h))
    pair = pl.BlockSpec((length, 2 * head_width), lambda h: (0, h))
    return pl.pallas_call(
        functools.partial(input_back_kernel, len(arrived)),
        grid=(heads,),
        in_specs=[
            full_spec(whole), full_spec((1, model)),
            full_spec((length, head_width)), full_spec((length, head_width)),
            column, pair, *[pair for _ in arrived],
            weight_at(0), weight_at(1), weight_at(2),
        ],
        out_specs=[column, column, full_spec(whole), full_spec((1, model))],
        out_shape=[
            jax.ShapeDtypeStruct((length, width), BF16),
            jax.ShapeDtypeStruct((length, width), BF16),
            jax.ShapeDtypeStruct(whole, BF16),
            jax.ShapeDtypeStruct((1, model), F32),
        ],
        scratch_shapes=[pltpu.VMEM(whole, F32)],
        cost_estimate=cost(6 * length * model * width, 6 * model * width + 16 * length * model),
        name="input_backward",
    )(x, gain, cos_table, sin_table, grad_q, own, *arrived, weights, weights, weights)


def tables(doc_lengths, length):
    doc_count = doc_lengths.shape[0]
    doc_ends = jnp.cumsum(doc_lengths)
    places = jnp.arange(length, dtype=jnp.int32)
    segment = jnp.sum((places[:, None] >= doc_ends[None, :]).astype(jnp.int32), axis=1)
    matched = segment[:, None] == jnp.arange(doc_count, dtype=jnp.int32)[None, :]
    doc_start = jnp.sum(jnp.where(matched, (doc_ends - doc_lengths)[None, :], 0), axis=1)
    return (segment, places - doc_start, segment < doc_count - 1)


def rotary(position, half_width):
    pair_count = half_width // 2
    frequency = jnp.exp(
        jnp.arange(pair_count, dtype=F32) * (-2.0 * math.log(10000.0) / half_width)
    )
    angles = position.astype(F32)[:, None] * frequency[None, :]
    cosine, sine = jnp.cos(angles), jnp.sin(angles)
    return (
        jnp.concatenate([cosine] * 4, axis=1),
        jnp.concatenate([-sine, sine, -sine, sine], axis=1),
    )


def other_half(part):
    count = lax.axis_size("mp")
    return lax.ppermute(part, "mp", [(i, (i + 1) % count) for i in range(count)])


def shift(values, step):
    count = lax.axis_size("seq")
    pairs = [(i, i + step) for i in range(count) if 0 <= i + step < count]
    return lax.ppermute(values, "seq", pairs)


def weight_grad(left, right):
    return dot_tn(left, right).astype(BF16)


def per_device(
    tokens, doc_lengths, attention_gain, query_weight, key_weight, value_weight, output_weight,
    head_gain, lambda_vectors, feedforward_gain, gate_weight, up_weight, down_weight, cotangent,
):
    local_len = tokens.shape[1]
    seq_count = lax.axis_size("seq")
    row_len = local_len * seq_count
    me = lax.axis_index("seq")
    offset = me * local_len
    half_width = lambda_vectors.shape[1]
    head_width = 2 * half_width
    width = query_weight.shape[1]
    heads = width // head_width
    hidden_units = gate_weight.shape[1]
    back_steps = min(seq_count - 1, -(-(MOST_DOC - 1) // local_len))
    whole = ("dp", "seq")

    attention_weights = lax.all_gather(
        jnp.concatenate([query_weight, key_weight, value_weight, output_weight], axis=1),
        whole, axis=0, tiled=True,
    )
    feed_weights = lax.all_gather(
        jnp.concatenate([gate_weight, up_weight, down_weight], axis=1), whole, axis=0, tiled=True
    )

    segment, position, usable = tables(doc_lengths[0], row_len)
    local_segment = lax.dynamic_slice_in_dim(segment, offset, local_len)
    local_position = lax.dynamic_slice_in_dim(position, offset, local_len)
    local_usable = lax.dynamic_slice_in_dim(usable, offset, local_len).astype(F32)[:, None]
    by_block = segment.reshape(seq_count, local_len)
    key_segments = []
    for b in range(back_steps + 1):
        rows = lax.dynamic_index_in_dim(by_block, jnp.maximum(me - b, 0), 0, keepdims=True)
        key_segments.append(jnp.where(me >= b, rows, -1))
    seg_k = jnp.concatenate(key_segments, axis=0)
    seg_q = local_segment[:, None]
    cos_table, sin_table = rotary(local_position, half_width)
    first_exp = jnp.exp(jnp.sum(lambda_vectors[0] * lambda_vectors[1]))
    second_exp = jnp.exp(jnp.sum(lambda_vectors[2] * lambda_vectors[3]))
    lam = (first_exp - second_exp + LAMBDA_INIT).reshape(1, 1)
    gain_one = attention_gain[None]
    gain_two = feedforward_gain[None]
    gain_head = head_gain[None]
    inputs = tokens[0]

    qkv, normed_one = project_qkv(
        inputs, gain_one, cos_table, sin_table, attention_weights, width, head_width
    )
    prior = [shift(qkv[:, width:], b) for b in range(1, back_steps + 1)]
    normed_head, mixture, second, logsum = attend(
        lam, seg_q, seg_k, gain_head, qkv, prior, heads, head_width
    )
    attention_part = lax.optimization_barrier(
        dot_nt(normed_head, attention_weights[:, 3 * width :]).astype(BF16)
    )
    (
        hidden, normed_two, grad_low, inner, grad_gate, grad_up, feed_part, feed_back,
        feed_gain_part,
    ) = feed_forward(
        inputs, attention_part, other_half(attention_part), gain_two, cotangent[0], local_usable,
        feed_weights, hidden_units,
    )
    outs = attend_back(
        lam, seg_q, seg_k, gain_head, cos_table, sin_table, grad_low, feed_back,
        other_half(feed_back), attention_weights, mixture, second, logsum, qkv, prior, heads,
        head_width,
    )
    grad_hidden, hidden_low, grad_q, own_kv = outs[:4]
    prior_kv = outs[4 : 4 + back_steps]
    head_gain_part, lambda_part = outs[4 + back_steps :]
    result = hidden + (feed_part.astype(F32) + other_half(feed_part).astype(F32))
    feed_grads = lax.psum_scatter(
        jnp.concatenate(
            [
                weight_grad(normed_two, grad_gate),
                weight_grad(normed_two, grad_up),
                weight_grad(grad_low, inner),
            ],
            axis=1,
        ),
        whole, scatter_dimension=0, tiled=True,
    ).astype(F32)
    arrived = [shift(values, -(b + 1)) for b, values in enumerate(prior_kv)]
    grad_k, grad_v, input_part, attention_gain_part = input_back(
        inputs, gain_one, cos_table, sin_table, grad_q, own_kv, arrived, attention_weights, heads,
        head_width,
    )
    attention_grads = lax.psum_scatter(
        jnp.concatenate(
            [
                weight_grad(normed_one, grad_q),
                weight_grad(normed_one, grad_k),
                weight_grad(normed_one, grad_v),
                weight_grad(hidden_low, normed_head),
            ],
            axis=1,
        ),
        whole, scatter_dimension=0, tiled=True,
    ).astype(F32)
    grad_tokens = grad_hidden + (input_part.astype(F32) + other_half(input_part).astype(F32))
    gain_sums = lax.psum(
        jnp.concatenate(
            [
                attention_gain_part[0], feed_gain_part[0], head_gain_part[0],
                jnp.sum(lambda_part).reshape(1),
            ]
        ),
        ("dp", "seq", "mp"),
    )
    model = inputs.shape[1]
    lambda_total = gain_sums[-1]
    lambda_grad = jnp.stack(
        [
            lambda_total * first_exp * lambda_vectors[1],
            lambda_total * first_exp * lambda_vectors[0],
            -lambda_total * second_exp * lambda_vectors[3],
            -lambda_total * second_exp * lambda_vectors[2],
        ]
    )
    return (
        result.astype(BF16)[None],
        grad_tokens.astype(BF16)[None],
        gain_sums[:model],
        attention_grads[:, :width],
        attention_grads[:, width : 2 * width],
        attention_grads[:, 2 * width : 3 * width],
        attention_grads[:, 3 * width :],
        gain_sums[2 * model : 2 * model + head_width],
        lambda_grad,
        gain_sums[model : 2 * model],
        feed_grads[:, :hidden_units],
        feed_grads[:, hidden_units : 2 * hidden_units],
        feed_grads[:, 2 * hidden_units :],
    )


def solution(mesh):
    rows = P(("dp", "seq"), "mp")
    activations = P("dp", "seq", None)
    in_specs = (
        activations, P("dp", None), P(), rows, rows, rows, rows, P(), P(), P(), rows, rows, rows,
        activations,
    )
    out_specs = (
        activations, activations, P(), rows, rows, rows, rows, P(), P(), P(), rows, rows, rows,
    )
    return jax.shard_map(
        per_device, mesh=mesh, in_specs=in_specs, out_specs=out_specs, check_vma=False
    )
```

```python
import functools
import math

import jax
import jax.numpy as jnp
from jax import lax
from jax.experimental import pallas as pl
from jax.experimental.pallas import tpu as pltpu
from jax.sharding import PartitionSpec as P

EPSILON = 1e-05
LAMBDA_INIT = 0.2
OUTPUT_SCALE = 1.0 - LAMBDA_INIT
NEGATIVE = -1e30
MOST_DOC = 512
F32 = jnp.float32
BF16 = jnp.bfloat16


def dot(a, b):
    return lax.dot_general(a, b, (((1,), (0,)), ((), ())), preferred_element_type=F32)


def dot_nt(a, b):
    return lax.dot_general(a, b, (((1,), (1,)), ((), ())), preferred_element_type=F32)


def dot_tn(a, b):
    return lax.dot_general(a, b, (((0,), (0,)), ((), ())), preferred_element_type=F32)


def full_spec(shape):
    return pl.BlockSpec(shape, lambda *_: (0,) * len(shape))


def cost(flops, moved, special=0):
    return pl.CostEstimate(flops=int(flops), bytes_accessed=int(moved), transcendentals=int(special))


def swap_halves(values, quarter):
    width = 4 * quarter
    lane = lax.broadcasted_iota(jnp.int32, values.shape, 1)
    ahead = pltpu.roll(values, width - quarter, 1)
    behind = pltpu.roll(values, quarter, 1)
    return jnp.where((lane % (2 * quarter)) < quarter, ahead, behind)


def qkv_kernel(rotated, head_width, x_ref, gain_ref, cos_ref, sin_ref, w_ref, out_ref, normed_ref):
    step = pl.program_id(0)

    @pl.when(step == 0)
    def _():
        values = x_ref[...].astype(F32)
        inverse = lax.rsqrt(jnp.mean(values * values, axis=-1, keepdims=True) + EPSILON)
        normed_ref[...] = (values * inverse * gain_ref[...]).astype(BF16)

    product = dot(normed_ref[...], w_ref[...])

    @pl.when(step < rotated)
    def _():
        for start in range(0, product.shape[1], head_width):
            piece = product[:, start : start + head_width]
            turned = piece * cos_ref[...] + swap_halves(piece, head_width // 4) * sin_ref[...]
            out_ref[:, start : start + head_width] = turned.astype(BF16)

    @pl.when(step >= rotated)
    def _():
        out_ref[...] = product.astype(BF16)


def project_qkv(x, gain, cos_table, sin_table, weights, width, head_width):
    length, model = x.shape
    tile = 256
    return pl.pallas_call(
        functools.partial(qkv_kernel, 2 * width // tile, head_width),
        grid=(3 * width // tile,),
        in_specs=[
            full_spec((length, model)),
            full_spec((1, model)),
            full_spec((length, head_width)),
            full_spec((length, head_width)),
            pl.BlockSpec((model, tile), lambda j: (0, j)),
        ],
        out_specs=[
            pl.BlockSpec((length, tile), lambda j: (0, j)),
            full_spec((length, model)),
        ],
        out_shape=[
            jax.ShapeDtypeStruct((length, 3 * width), BF16),
            jax.ShapeDtypeStruct((length, model), BF16),
        ],
        cost_estimate=cost(6 * length * model * width, 6 * model * width + 8 * length * width),
        name="qkv_project",
    )(x, gain, cos_table, sin_table, weights)


def masks_of(seg_q, seg_k_ref, blocks):
    length = seg_q.shape[0]
    allowed = []
    for b in range(blocks):
        same = seg_q == seg_k_ref[b : b + 1, :]
        if b == 0:
            rows = lax.broadcasted_iota(jnp.int32, (length, length), 0)
            columns = lax.broadcasted_iota(jnp.int32, (length, length), 1)
            same = same & (rows >= columns)
        allowed.append(same)
    return allowed


def attend_kernel(blocks, *refs):
    lam_ref, seg_q_ref, seg_k_ref, gain_ref, q_ref = refs[:5]
    k_refs = refs[5 : 5 + blocks]
    v_refs = refs[5 + blocks : 5 + 2 * blocks]
    normed_ref, mixture_ref, second_ref, logsum_ref = refs[5 + 2 * blocks :]
    half = q_ref.shape[1] // 2
    scale = half ** (-0.5)
    allowed = masks_of(seg_q_ref[...], seg_k_ref, blocks)
    outputs = []
    for j in range(2):
        cut = slice(j * half, (j + 1) * half)
        query = q_ref[:, cut]
        scores = [
            jnp.where(allowed[b], dot_nt(query, k_refs[b][:, cut]) * scale, NEGATIVE)
            for b in range(blocks)
        ]
        highest = functools.reduce(
            jnp.maximum, [jnp.max(s, axis=-1, keepdims=True) for s in scores]
        )
        exponents = [jnp.exp(s - highest) for s in scores]
        total = sum(jnp.sum(e, axis=-1, keepdims=True) for e in exponents)
        inverse = 1.0 / total
        outputs.append(
            sum(dot((exponents[b] * inverse).astype(BF16), v_refs[b][...]) for b in range(blocks))
        )
        logsum_ref[0, :, j : j + 1] = highest + jnp.log(total)
    mixture = outputs[0] - lam_ref[0, 0] * outputs[1]
    inverse_head = lax.rsqrt(jnp.mean(mixture * mixture, axis=-1, keepdims=True) + EPSILON)
    normed_ref[...] = (mixture * inverse_head * (gain_ref[...] * OUTPUT_SCALE)).astype(BF16)
    mixture_ref[...] = mixture
    second_ref[...] = outputs[1]


def attend(lam, seg_q, seg_k, head_gain, qkv, prior, heads, head_width):
    length = qkv.shape[0]
    blocks = seg_k.shape[0]
    block = (length, head_width)

    def at(first):
        return pl.BlockSpec(block, lambda h: (0, first + h))

    width = heads * head_width
    return pl.pallas_call(
        functools.partial(attend_kernel, blocks),
        grid=(heads,),
        in_specs=[
            pl.BlockSpec(memory_space=pltpu.SMEM),
            full_spec(seg_q.shape),
            full_spec(seg_k.shape),
            full_spec(head_gain.shape),
            at(0),
            at(heads),
            *[at(0) for _ in prior],
            at(2 * heads),
            *[at(heads) for _ in prior],
        ],
        out_specs=[at(0), at(0), at(0), pl.BlockSpec((1, length, 2), lambda h: (h, 0, 0))],
        out_shape=[
            jax.ShapeDtypeStruct((length, width), BF16),
            jax.ShapeDtypeStruct((length, width), F32),
            jax.ShapeDtypeStruct((length, width), F32),
            jax.ShapeDtypeStruct((heads, length, 2), F32),
        ],
        cost_estimate=cost(
            8 * heads * length * length * blocks * head_width,
            length * width * (2 + 4 * blocks + 10),
            2 * heads * length * length * blocks,
        ),
        name="attend_forward",
    )(lam, seg_q, seg_k, head_gain, qkv, qkv, *prior, qkv, *prior)


def feed_kernel(
    x_ref, own_ref, other_ref, gain_ref, cot_ref, usable_ref, gate_ref, up_ref, down_ref,
    hidden_ref, normed_ref, low_ref, inner_ref, grad_gate_ref, grad_up_ref,
    part_ref, back_ref, gain_part_ref, sum_out, sum_back, inverse_ref,
):
    step = pl.program_id(0)
    gain = gain_ref[...]

    @pl.when(step == 0)
    def _():
        hidden = x_ref[...].astype(F32) + (own_ref[...].astype(F32) + other_ref[...].astype(F32))
        inverse = lax.rsqrt(jnp.mean(hidden * hidden, axis=-1, keepdims=True) + EPSILON)
        hidden_ref[...] = hidden
        inverse_ref[...] = inverse
        normed_ref[...] = (hidden * inverse * gain).astype(BF16)
        low_ref[...] = (cot_ref[...].astype(F32) * usable_ref[...]).astype(BF16)
        sum_out[...] = jnp.zeros_like(sum_out)
        sum_back[...] = jnp.zeros_like(sum_back)

    normed = normed_ref[...]
    gate = dot(normed, gate_ref[...])
    up = dot(normed, up_ref[...])
    grad_inner = dot(low_ref[...], down_ref[...])
    sigmoid = jax.nn.sigmoid(gate)
    silu = gate * sigmoid
    inner = (silu * up).astype(BF16)
    grad_gate = (grad_inner * up * (sigmoid * (1.0 + gate * (1.0 - sigmoid)))).astype(BF16)
    grad_up = (grad_inner * silu).astype(BF16)
    inner_ref[...] = inner
    grad_gate_ref[...] = grad_gate
    grad_up_ref[...] = grad_up
    sum_out[...] += dot_nt(inner, down_ref[...])
    sum_back[...] += dot_nt(grad_gate, gate_ref[...]) + dot_nt(grad_up, up_ref[...])

    @pl.when(step == pl.num_programs(0) - 1)
    def _():
        part_ref[...] = sum_out[...].astype(BF16)
        inverse = inverse_ref[...]
        unit = hidden_ref[...] * inverse
        grad = sum_back[...]
        weighed = gain * grad
        gain_part_ref[...] = jnp.sum(grad * unit, axis=0, keepdims=True)
        centre = jnp.mean(weighed * unit, axis=-1, keepdims=True)
        back_ref[...] = (inverse * (weighed - unit * centre)).astype(BF16)


def feed_forward(x, own, other, gain, cotangent, usable, weights, hidden_units):
    length, model = x.shape
    tile = 256
    tiles = hidden_units // tile
    whole = (length, model)

    def weight_at(first):
        return pl.BlockSpec((model, tile), lambda j: (0, first * tiles + j))

    column = pl.BlockSpec((length, tile), lambda j: (0, j))
    return pl.pallas_call(
        feed_kernel,
        grid=(tiles,),
        in_specs=[
            full_spec(whole), full_spec(whole), full_spec(whole), full_spec((1, model)),
            full_spec(whole), full_spec((length, 1)), weight_at(0), weight_at(1), weight_at(2),
        ],
        out_specs=[
            full_spec(whole), full_spec(whole), full_spec(whole), column, column, column,
            full_spec(whole), full_spec(whole), full_spec((1, model)),
        ],
        out_shape=[
            jax.ShapeDtypeStruct(whole, F32),
            jax.ShapeDtypeStruct(whole, BF16),
            jax.ShapeDtypeStruct(whole, BF16),
            *[jax.ShapeDtypeStruct((length, hidden_units), BF16)] * 3,
            jax.ShapeDtypeStruct(whole, BF16),
            jax.ShapeDtypeStruct(whole, BF16),
            jax.ShapeDtypeStruct((1, model), F32),
        ],
        scratch_shapes=[
            pltpu.VMEM(whole, F32), pltpu.VMEM(whole, F32), pltpu.VMEM((length, 1), F32),
        ],
        cost_estimate=cost(
            12 * length * model * hidden_units, 6 * model * hidden_units + 20 * length * model
        ),
        name="feed_forward",
    )(x, own, other, gain, cotangent, usable, weights, weights, weights)


def attend_back_kernel(blocks, *refs):
    (lam_ref, seg_q_ref, seg_k_ref, gain_ref, cos_ref, sin_ref, low_ref, own_ref, other_ref,
     out_weight_ref, mixture_ref, second_ref, logsum_ref, q_ref) = refs[:14]
    k_refs = refs[14 : 14 + blocks]
    v_refs = refs[14 + blocks : 14 + 2 * blocks]
    grad_hidden_ref, hidden_low_ref, grad_q_ref, own_kv_ref = refs[14 + 2 * blocks : 18 + 2 * blocks]
    prior_kv_refs = refs[18 + 2 * blocks : 17 + 3 * blocks]
    gain_part_ref, lam_part_ref = refs[17 + 3 * blocks :]
    step = pl.program_id(0)

    @pl.when(step == 0)
    def _():
        grad_hidden = low_ref[...].astype(F32) + (
            own_ref[...].astype(F32) + other_ref[...].astype(F32)
        )
        grad_hidden_ref[...] = grad_hidden
        hidden_low_ref[...] = grad_hidden.astype(BF16)
        gain_part_ref[...] = jnp.zeros_like(gain_part_ref)
        lam_part_ref[...] = jnp.zeros_like(lam_part_ref)

    head_width = q_ref.shape[1]
    half = head_width // 2
    scale = half ** (-0.5)
    lam = lam_ref[0, 0]
    grad_head = dot(hidden_low_ref[...], out_weight_ref[...])
    mixture = mixture_ref[...]
    inverse_head = lax.rsqrt(jnp.mean(mixture * mixture, axis=-1, keepdims=True) + EPSILON)
    unit_head = mixture * inverse_head
    gain_part_ref[...] += jnp.sum(grad_head * unit_head, axis=0, keepdims=True) * OUTPUT_SCALE
    weighed = gain_ref[...] * OUTPUT_SCALE * grad_head
    centre_head = jnp.mean(weighed * unit_head, axis=-1, keepdims=True)
    grad_mixture = inverse_head * (weighed - unit_head * centre_head)
    lam_part_ref[...] -= jnp.sum(grad_mixture * second_ref[...], axis=0, keepdims=True)
    grads = (grad_mixture.astype(BF16), (-lam * grad_mixture).astype(BF16))
    allowed = masks_of(seg_q_ref[...], seg_k_ref, blocks)
    grad_queries = []
    grad_keys = [[] for _ in range(blocks)]
    grad_values = [0.0] * blocks
    for j in range(2):
        cut = slice(j * half, (j + 1) * half)
        query = q_ref[:, cut]
        grad_out = grads[j]
        logsum = logsum_ref[0, :, j : j + 1]
        soft, grad_soft = [], []
        for b in range(blocks):
            scores = dot_nt(query, k_refs[b][:, cut]) * scale
            soft.append(jnp.exp(jnp.where(allowed[b], scores - logsum, NEGATIVE)))
            grad_soft.append(dot_nt(grad_out, v_refs[b][...]))
            grad_values[b] = grad_values[b] + dot_tn(soft[b].astype(BF16), grad_out)
        centre = sum(jnp.sum(soft[b] * grad_soft[b], axis=-1, keepdims=True) for b in range(blocks))
        grad_query = 0.0
        for b in range(blocks):
            grad_scores = (scale * soft[b] * (grad_soft[b] - centre)).astype(BF16)
            grad_query = grad_query + dot(grad_scores, k_refs[b][:, cut])
            grad_keys[b].append(dot_tn(grad_scores, query))
        grad_queries.append(grad_query)
    grad_query = jnp.concatenate(grad_queries, axis=1)
    turned = grad_query * cos_ref[...] - swap_halves(grad_query, head_width // 4) * sin_ref[...]
    grad_q_ref[...] = turned.astype(BF16)
    for b, ref in enumerate((own_kv_ref, *prior_kv_refs)):
        ref[:, :head_width] = jnp.concatenate(grad_keys[b], axis=1).astype(ref.dtype)
        ref[:, head_width:] = grad_values[b].astype(ref.dtype)


def attend_back(
    lam, seg_q, seg_k, head_gain, cos_table, sin_table, grad_low, own, other, weights,
    mixture, second, logsum, qkv, prior, heads, head_width,
):
    length, model = grad_low.shape
    blocks = seg_k.shape[0]
    whole = (length, model)
    width = heads * head_width

    def at(first):
        return pl.BlockSpec((length, head_width), lambda h: (0, first + h))

    pair = pl.BlockSpec((length, 2 * head_width), lambda h: (0, h))
    return pl.pallas_call(
        functools.partial(attend_back_kernel, blocks),
        grid=(heads,),
        in_specs=[
            pl.BlockSpec(memory_space=pltpu.SMEM),
            full_spec(seg_q.shape), full_spec(seg_k.shape), full_spec(head_gain.shape),
            full_spec((length, head_width)), full_spec((length, head_width)),
            full_spec(whole), full_spec(whole), full_spec(whole),
            pl.BlockSpec((model, head_width), lambda h: (0, 3 * heads + h)),
            at(0), at(0), pl.BlockSpec((1, length, 2), lambda h: (h, 0, 0)),
            at(0),
            at(heads), *[at(0) for _ in prior],
            at(2 * heads), *[at(heads) for _ in prior],
        ],
        out_specs=[
            full_spec(whole), full_spec(whole), at(0), pair, *[pair for _ in prior],
            full_spec((1, head_width)), full_spec((1, head_width)),
        ],
        out_shape=[
            jax.ShapeDtypeStruct(whole, F32),
            jax.ShapeDtypeStruct(whole, BF16),
            jax.ShapeDtypeStruct((length, width), BF16),
            jax.ShapeDtypeStruct((length, 2 * width), F32),
            *[jax.ShapeDtypeStruct((length, 2 * width), BF16) for _ in prior],
            jax.ShapeDtypeStruct((1, head_width), F32),
            jax.ShapeDtypeStruct((1, head_width), F32),
        ],
        cost_estimate=cost(
            24 * heads * length * length * blocks * head_width + 2 * length * model * width,
            2 * model * width + 24 * length * model,
            2 * heads * length * length * blocks,
        ),
        name="attend_backward",
    )(
        lam, seg_q, seg_k, head_gain, cos_table, sin_table, grad_low, own, other, weights,
        mixture, second, logsum, qkv, qkv, *prior, qkv, *prior,
    )


def input_back_kernel(
    arrivals, *refs,
):
    x_ref, gain_ref, cos_ref, sin_ref, grad_q_ref, own_ref = refs[:6]
    arrival_refs = refs[6 : 6 + arrivals]
    wq_ref, wk_ref, wv_ref, grad_k_ref, grad_v_ref, back_ref, gain_part_ref, total = refs[6 + arrivals :]
    step = pl.program_id(0)
    head_width = grad_q_ref.shape[1]
    pair = own_ref[...]
    for ref in arrival_refs:
        pair = pair + ref[...].astype(F32)
    grad_key = pair[:, :head_width]
    turned = grad_key * cos_ref[...] - swap_halves(grad_key, head_width // 4) * sin_ref[...]
    grad_k = turned.astype(BF16)
    grad_v = pair[:, head_width:].astype(BF16)
    grad_k_ref[...] = grad_k
    grad_v_ref[...] = grad_v

    @pl.when(step == 0)
    def _():
        total[...] = jnp.zeros_like(total)

    total[...] += (
        dot_nt(grad_q_ref[...], wq_ref[...])
        + dot_nt(grad_k, wk_ref[...])
        + dot_nt(grad_v, wv_ref[...])
    )

    @pl.when(step == pl.num_programs(0) - 1)
    def _():
        values = x_ref[...].astype(F32)
        inverse = lax.rsqrt(jnp.mean(values * values, axis=-1, keepdims=True) + EPSILON)
        unit = values * inverse
        grad = total[...]
        weighed = gain_ref[...] * grad
        gain_part_ref[...] = jnp.sum(grad * unit, axis=0, keepdims=True)
        centre = jnp.mean(weighed * unit, axis=-1, keepdims=True)
        back_ref[...] = (inverse * (weighed - unit * centre)).astype(BF16)


def input_back(x, gain, cos_table, sin_table, grad_q, own, arrived, weights, heads, head_width):
    length, model = x.shape
    width = heads * head_width
    whole = (length, model)

    def weight_at(first):
        return pl.BlockSpec((model, head_width), lambda h: (0, first * heads + h))

    column = pl.BlockSpec((length, head_width), lambda h: (0, h))
    pair = pl.BlockSpec((length, 2 * head_width), lambda h: (0, h))
    return pl.pallas_call(
        functools.partial(input_back_kernel, len(arrived)),
        grid=(heads,),
        in_specs=[
            full_spec(whole), full_spec((1, model)),
            full_spec((length, head_width)), full_spec((length, head_width)),
            column, pair, *[pair for _ in arrived],
            weight_at(0), weight_at(1), weight_at(2),
        ],
        out_specs=[column, column, full_spec(whole), full_spec((1, model))],
        out_shape=[
            jax.ShapeDtypeStruct((length, width), BF16),
            jax.ShapeDtypeStruct((length, width), BF16),
            jax.ShapeDtypeStruct(whole, BF16),
            jax.ShapeDtypeStruct((1, model), F32),
        ],
        scratch_shapes=[pltpu.VMEM(whole, F32)],
        cost_estimate=cost(6 * length * model * width, 6 * model * width + 16 * length * model),
        name="input_backward",
    )(x, gain, cos_table, sin_table, grad_q, own, *arrived, weights, weights, weights)


def tables(doc_lengths, length):
    doc_count = doc_lengths.shape[0]
    doc_ends = jnp.cumsum(doc_lengths)
    places = jnp.arange(length, dtype=jnp.int32)
    segment = jnp.sum((places[:, None] >= doc_ends[None, :]).astype(jnp.int32), axis=1)
    matched = segment[:, None] == jnp.arange(doc_count, dtype=jnp.int32)[None, :]
    doc_start = jnp.sum(jnp.where(matched, (doc_ends - doc_lengths)[None, :], 0), axis=1)
    return (segment, places - doc_start, segment < doc_count - 1)


def rotary(position, half_width):
    pair_count = half_width // 2
    frequency = jnp.exp(
        jnp.arange(pair_count, dtype=F32) * (-2.0 * math.log(10000.0) / half_width)
    )
    angles = position.astype(F32)[:, None] * frequency[None, :]
    cosine, sine = jnp.cos(angles), jnp.sin(angles)
    return (
        jnp.concatenate([cosine] * 4, axis=1),
        jnp.concatenate([-sine, sine, -sine, sine], axis=1),
    )


def other_half(part):
    count = lax.axis_size("mp")
    return lax.ppermute(part, "mp", [(i, (i + 1) % count) for i in range(count)])


def shift(values, step):
    count = lax.axis_size("seq")
    pairs = [(i, i + step) for i in range(count) if 0 <= i + step < count]
    return lax.ppermute(values, "seq", pairs)


def flip(values, bit):
    count = lax.axis_size("seq")
    return lax.ppermute(values, "seq", [(i, i ^ bit) for i in range(count)])


def everyone_sum(values):
    for axis in ("mp", "seq", "dp"):
        count = lax.axis_size(axis)
        if count & (count - 1):
            values = lax.psum(values, axis)
            continue
        bit = 1
        while bit < count:
            values = values + lax.ppermute(values, axis, [(i, i ^ bit) for i in range(count)])
            bit *= 2
    return values


def split_grad_kernel(counts, dp_count, dp_major, rows, me_ref, *refs):
    pairs = len(counts)
    lefts, rights = refs[:pairs], refs[pairs : 2 * pairs]
    send_ref, keep_ref = refs[2 * pairs :]
    step = pl.program_id(0)
    core = me_ref[0, 0] % 2
    side = (me_ref[0, 0] // 2) % 2
    start = 0
    for left_ref, right_ref, count in zip(lefts, rights, counts):

        @pl.when((step >= start) & (step < start + count))
        def _(left_ref=left_ref, right_ref=right_ref):
            product = dot_tn(left_ref[...], right_ref[...]).astype(BF16)
            for d in range(dp_count):
                for x in range(2):
                    first = (d * 4 + x * 2) * rows
                    even = product[first : first + rows]
                    odd = product[first + rows : first + 2 * rows]
                    mine = (side == x).astype(jnp.int32)
                    if dp_major:
                        place = (2 * d + mine) * rows
                    else:
                        place = (mine * dp_count + d) * rows
                    spot = pl.ds(pl.multiple_of(place, rows), rows)
                    send_ref[spot, :] = jnp.where(core == 0, odd, even)
                    keep_ref[spot, :] = jnp.where(core == 0, even, odd)

        start += count


def split_grads(me, pairs, dp_count, dp_major):
    length, model = pairs[0][0].shape
    tile = 256
    counts = tuple(right.shape[1] // tile for _, right in pairs)
    starts = [sum(counts[:i]) for i in range(len(counts))]
    width = tile * sum(counts)
    rows = model // (4 * dp_count)

    def right_spec(start, count):
        return pl.BlockSpec((length, tile), lambda j: (0, jnp.clip(j - start, 0, count - 1)))

    column = pl.BlockSpec((model // 2, tile), lambda j: (0, j))
    return pl.pallas_call(
        functools.partial(split_grad_kernel, counts, dp_count, dp_major, rows),
        grid=(sum(counts),),
        in_specs=[
            pl.BlockSpec(memory_space=pltpu.SMEM),
            *[full_spec((length, model)) for _ in pairs],
            *[right_spec(start, count) for start, count in zip(starts, counts)],
        ],
        out_specs=[column, column],
        out_shape=[jax.ShapeDtypeStruct((model // 2, width), BF16)] * 2,
        cost_estimate=cost(2 * length * model * width, 2 * model * width + 4 * length * width),
        name="weight_grads",
    )(me, *[left for left, _ in pairs], *[right for _, right in pairs])


def add(first, second):
    return first.astype(F32) + second.astype(F32)


def staged_scatter(me, pairs, order):
    dp_count = lax.axis_size("dp")
    send, keep = split_grads(me.reshape(1, 1), pairs, dp_count, order == "dp_first")
    arrived = flip(send, 1)
    if order == "dp_first":
        total = lax.psum_scatter(
            add(keep, arrived).astype(BF16), "dp", scatter_dimension=0, tiled=True
        )
        half = total.shape[0] // 2
        return add(total[half:], flip(total[:half], 2))
    half = keep.shape[0] // 2
    away = flip(add(keep[:half], arrived[:half]).astype(BF16), 2)
    total = add(keep[half:], arrived[half:]) + away.astype(F32)
    if order == "queue":
        total = total.astype(BF16)
        return lax.psum_scatter(total, "dp", scatter_dimension=0, tiled=True).astype(F32)
    by_owner = total.astype(BF16).reshape(dp_count, half // dp_count, -1)
    place = lax.axis_index("dp")
    result = lax.dynamic_index_in_dim(by_owner, place, 0, keepdims=False).astype(F32)
    for step in range(1, dp_count):
        chunk = lax.dynamic_index_in_dim(by_owner, (place + step) % dp_count, 0, keepdims=False)
        hops = [(i, (i + step) % dp_count) for i in range(dp_count)]
        result = result + lax.ppermute(chunk, "dp", hops).astype(F32)
    return result


def plain_scatter(pairs):
    grads = [dot_tn(left, right).astype(BF16) for left, right in pairs]
    return lax.psum_scatter(
        jnp.concatenate(grads, axis=1), ("dp", "seq"), scatter_dimension=0, tiled=True
    ).astype(F32)


def per_device(
    tokens, doc_lengths, attention_gain, query_weight, key_weight, value_weight, output_weight,
    head_gain, lambda_vectors, feedforward_gain, gate_weight, up_weight, down_weight, cotangent,
):
    local_len = tokens.shape[1]
    seq_count = lax.axis_size("seq")
    row_len = local_len * seq_count
    me = lax.axis_index("seq")
    offset = me * local_len
    half_width = lambda_vectors.shape[1]
    head_width = 2 * half_width
    width = query_weight.shape[1]
    heads = width // head_width
    hidden_units = gate_weight.shape[1]
    back_steps = min(seq_count - 1, -(-(MOST_DOC - 1) // local_len))
    whole = ("dp", "seq")

    attention_weights = lax.all_gather(
        jnp.concatenate([query_weight, key_weight, value_weight, output_weight], axis=1),
        whole, axis=0, tiled=True,
    )
    feed_weights = lax.all_gather(
        jnp.concatenate([gate_weight, up_weight, down_weight], axis=1), whole, axis=0, tiled=True
    )

    segment, position, usable = tables(doc_lengths[0], row_len)
    local_segment = lax.dynamic_slice_in_dim(segment, offset, local_len)
    local_position = lax.dynamic_slice_in_dim(position, offset, local_len)
    local_usable = lax.dynamic_slice_in_dim(usable, offset, local_len).astype(F32)[:, None]
    by_block = segment.reshape(seq_count, local_len)
    key_segments = []
    for b in range(back_steps + 1):
        rows = lax.dynamic_index_in_dim(by_block, jnp.maximum(me - b, 0), 0, keepdims=True)
        key_segments.append(jnp.where(me >= b, rows, -1))
    seg_k = jnp.concatenate(key_segments, axis=0)
    seg_q = local_segment[:, None]
    cos_table, sin_table = rotary(local_position, half_width)
    first_exp = jnp.exp(jnp.sum(lambda_vectors[0] * lambda_vectors[1]))
    second_exp = jnp.exp(jnp.sum(lambda_vectors[2] * lambda_vectors[3]))
    lam = (first_exp - second_exp + LAMBDA_INIT).reshape(1, 1)
    gain_one = attention_gain[None]
    gain_two = feedforward_gain[None]
    gain_head = head_gain[None]
    inputs = tokens[0]

    qkv, normed_one = project_qkv(
        inputs, gain_one, cos_table, sin_table, attention_weights, width, head_width
    )
    prior = [shift(qkv[:, width:], b) for b in range(1, back_steps + 1)]
    normed_head, mixture, second, logsum = attend(
        lam, seg_q, seg_k, gain_head, qkv, prior, heads, head_width
    )
    attention_part = lax.optimization_barrier(
        dot_nt(normed_head, attention_weights[:, 3 * width :]).astype(BF16)
    )
    (
        hidden, normed_two, grad_low, inner, grad_gate, grad_up, feed_part, feed_back,
        feed_gain_part,
    ) = feed_forward(
        inputs, attention_part, other_half(attention_part), gain_two, cotangent[0], local_usable,
        feed_weights, hidden_units,
    )
    outs = attend_back(
        lam, seg_q, seg_k, gain_head, cos_table, sin_table, grad_low, feed_back,
        other_half(feed_back), attention_weights, mixture, second, logsum, qkv, prior, heads,
        head_width,
    )
    grad_hidden, hidden_low, grad_q, own_kv = outs[:4]
    prior_kv = outs[4 : 4 + back_steps]
    head_gain_part, lambda_part = outs[4 + back_steps :]
    result = hidden + (feed_part.astype(F32) + other_half(feed_part).astype(F32))
    model = inputs.shape[1]
    staged = seq_count == 4 and model % (32 * 4 * lax.axis_size("dp")) == 0

    def scatter(pairs, order):
        return staged_scatter(me, pairs, order) if staged else plain_scatter(pairs)

    down_grad = scatter([(grad_low, inner)], "direct")
    up_grad = scatter([(normed_two, grad_up)], "queue")
    gate_grad = scatter([(normed_two, grad_gate)], "dp_first")
    query_out_grad = scatter([(normed_one, grad_q), (hidden_low, normed_head)], "queue")
    arrived = [shift(values, -(b + 1)) for b, values in enumerate(prior_kv)]
    grad_k, grad_v, input_part, attention_gain_part = input_back(
        inputs, gain_one, cos_table, sin_table, grad_q, own_kv, arrived, attention_weights, heads,
        head_width,
    )
    key_value_grad = scatter([(normed_one, grad_k), (normed_one, grad_v)], "direct")
    grad_tokens = grad_hidden + (input_part.astype(F32) + other_half(input_part).astype(F32))
    gain_sums = everyone_sum(
        jnp.concatenate([attention_gain_part, feed_gain_part, head_gain_part, lambda_part], axis=1)
    )[0]
    lambda_total = jnp.sum(gain_sums[-head_width:])
    lambda_grad = jnp.stack(
        [
            lambda_total * first_exp * lambda_vectors[1],
            lambda_total * first_exp * lambda_vectors[0],
            -lambda_total * second_exp * lambda_vectors[3],
            -lambda_total * second_exp * lambda_vectors[2],
        ]
    )
    return (
        result.astype(BF16)[None],
        grad_tokens.astype(BF16)[None],
        gain_sums[:model],
        query_out_grad[:, :width],
        key_value_grad[:, :width],
        key_value_grad[:, width:],
        query_out_grad[:, width:],
        gain_sums[2 * model : 2 * model + head_width],
        lambda_grad,
        gain_sums[model : 2 * model],
        gate_grad,
        up_grad,
        down_grad,
    )


def solution(mesh):
    rows = P(("dp", "seq"), "mp")
    activations = P("dp", "seq", None)
    in_specs = (
        activations, P("dp", None), P(), rows, rows, rows, rows, P(), P(), P(), rows, rows, rows,
        activations,
    )
    out_specs = (
        activations, activations, P(), rows, rows, rows, rows, P(), P(), P(), rows, rows, rows,
    )
    return jax.shard_map(
        per_device, mesh=mesh, in_specs=in_specs, out_specs=out_specs, check_vma=False
    )
```
